256 devices in a mesh: ctx: 32 (over x, z), head: 8 (over y, core).
Axes of the slice: x: 4, y: 4, z: 8, core: 2. Of those that a mesh axis runs over, the one named last changes fastest.
Arguments:
- queries: bfloat16 [65536, 4096], P('ctx', 'head'), may hold values from -28 to 28
- keys: bfloat16 [65536, 1024], P('ctx', 'head'), may hold values from -13 to 13
- values: bfloat16 [65536, 1024], P('ctx', 'head'), may hold values from -6 to 6
- vertical: int32 [8, 16], P('head'), may hold values from 0 to 1023, as said below
- slash: int32 [8, 8], P('head'), may hold values from 0 to 63, as said below
Outputs:
- attention: bfloat16 [65536, 4096], P(('ctx', 'head'))
The draws below stay inside these ranges and needn't reach their ends.
Inputs may be any that keep to these rules, and one draw needn't show every extreme that they name: `vertical`: each row lists 16 different blocks; at most 4 of one row lie within one index of ctx (2048 tokens), and exactly 4 do in some index. `slash`: each row lists 8 different offsets, 0 and 2 * 32 - 1 among them.
All inputs are finite; a program needn't handle non-finite values.
Results may differ from the reference program's by a relative error of at most 0.0043.
Values may be sent and summed in bfloat16 or wider, within the bound.
A program may use at most 64 MiB of HBM per device.

```python
import math
import jax
import jax.numpy as jnp
from jax import lax

HD = 128
KVH = 8
QH = 32
BLK = 64
TOK_DEV = 2048
NV = 16
NS = 8
MOWN = 4
LOOK = 2
HQ = 4
TOKENS = 65536
N_CTX = 32


def shared_draw(key):
    query_draw = jnp.clip(jax.random.normal(jax.random.fold_in(key, 101), (TOKENS, KVH, HQ, HD), jnp.float32), -5.0, 5.0)
    key_draw = jnp.clip(jax.random.normal(jax.random.fold_in(key, 102), (TOKENS, KVH, HD), jnp.float32), -5.0, 5.0)
    return (query_draw.reshape(TOKENS, KVH * HQ * HD), key_draw.reshape(TOKENS, KVH * HD))


def draw_queries(key, part):
    return shared_draw(key)[0].astype(jnp.bfloat16)


def draw_keys(key, part):
    return shared_draw(key)[1].astype(jnp.bfloat16)


def draw_vertical(key, part):
    blocks_dev = TOK_DEV // BLK
    heavy = jax.random.randint(jax.random.fold_in(key, 11), (KVH,), 0, N_CTX)

    def one_head(head_key, heavy_shard):
        heavy_local = jax.random.permutation(jax.random.fold_in(head_key, 1), blocks_dev)[:MOWN]
        heavy_blocks = heavy_shard * blocks_dev + heavy_local
        others = jax.random.permutation(jax.random.fold_in(head_key, 2), N_CTX - 1)
        spread = jax.random.permutation(jax.random.fold_in(head_key, 3), blocks_dev)
        positions = jnp.arange(NV - MOWN)
        shard_ids = (heavy_shard + 1 + others[positions % (N_CTX - 1)]) % N_CTX
        local_ids = spread[positions // (N_CTX - 1)]
        light_blocks = shard_ids * blocks_dev + local_ids
        listed = jnp.concatenate([heavy_blocks, light_blocks])
        return listed[jax.random.permutation(jax.random.fold_in(head_key, 4), NV)]
    head_keys = jax.random.split(jax.random.fold_in(key, 12), KVH)
    return jax.vmap(one_head)(head_keys, heavy).astype(jnp.int32)


def draw_slash(key, part):
    span_blocks = LOOK * (TOK_DEV // BLK)

    def one_head(head_key):
        middle = jax.random.permutation(head_key, span_blocks - 2)[:NS - 2] + 1
        return jnp.concatenate([jnp.zeros((1,), jnp.int32), jnp.full((1,), span_blocks - 1, jnp.int32), middle.astype(jnp.int32)])
    head_keys = jax.random.split(jax.random.fold_in(key, 21), KVH)
    return jax.vmap(one_head)(head_keys).astype(jnp.int32)


def levels(stream_key, shape, pieces, low, largest):
    def one(axis_at, parts):
        draws = jax.random.uniform(jax.random.fold_in(jax.random.fold_in(stream_key, 6), axis_at), (parts,), jnp.float32, low / len(pieces), largest / len(pieces))
        return jnp.repeat(jnp.exp(draws), shape[axis_at] // parts).reshape((-1,) + (1,) * (len(shape) - axis_at - 1))

    loudness = one(*pieces[0])
    for cut in pieces[1:]:
        loudness = loudness * one(*cut)
    return loudness


def normal_values(key, dims, scale, limit, pieces=(), kind=jnp.bfloat16):
    values = jax.random.normal(key, dims, jnp.float32) * scale
    if len(pieces) > 0:
        values = levels(key, dims, pieces, -0.22, 0.18) * values
    return jnp.clip(values, min=-limit, max=limit).astype(kind)


def setup_inputs(seed: int = 0) -> dict:
    key_of = jax.random.split(jax.random.key(seed), 6)
    return {
        "queries": draw_queries(jax.random.fold_in(key_of[5], 71), 0),
        "keys": draw_keys(jax.random.fold_in(key_of[5], 71), 0),
        "values": normal_values(key_of[2], (TOKENS, KVH * HD), 1.0, 6.0, ((0, 32), (1, 8))),
        "vertical": draw_vertical(jax.random.fold_in(key_of[5], 71), 0),
        "slash": draw_slash(jax.random.fold_in(key_of[5], 71), 0),
    }


def reference(queries, keys, values, vertical, slash):
    block_count = TOKENS // BLK
    group_heads = QH // KVH
    score_scale = 1.0 / math.sqrt(HD)
    query_blocks = queries.reshape(block_count, BLK, KVH, group_heads, HD)
    key_blocks = keys.reshape(block_count, BLK, KVH, HD)
    value_blocks = values.reshape(block_count, BLK, KVH, HD)
    offsets = jnp.arange(BLK).astype(jnp.int32)

    def attend_head(head_index):
        head_keys = jnp.take(key_blocks, head_index, axis=2)
        head_values = jnp.take(value_blocks, head_index, axis=2)
        head_queries = jnp.take(query_blocks, head_index, axis=2)
        vert_blocks = jnp.take(vertical, head_index, axis=0)
        slash_offsets = jnp.take(slash, head_index, axis=0)
        vert_keys = jnp.take(head_keys, vert_blocks, axis=0).reshape(NV * BLK, HD)
        vert_values = jnp.take(head_values, vert_blocks, axis=0).reshape(NV * BLK, HD)
        vert_pos = (vert_blocks[:, None] * BLK + offsets[None, :]).reshape(NV * BLK)

        def attend_block(block_index):
            query_rows = jnp.take(head_queries, block_index, axis=0)
            query_pos = block_index * BLK + offsets
            slash_blocks = block_index - slash_offsets
            safe_blocks = jnp.maximum(slash_blocks, 0)
            slash_keys = jnp.take(head_keys, safe_blocks, axis=0).reshape(NS * BLK, HD)
            slash_values = jnp.take(head_values, safe_blocks, axis=0).reshape(NS * BLK, HD)
            in_vertical = jnp.any(slash_blocks[:, None] == vert_blocks[None, :], axis=1)
            slash_valid = (slash_blocks >= 0) & jnp.logical_not(in_vertical)
            slash_pos = (slash_blocks[:, None] * BLK + offsets[None, :]).reshape(NS * BLK)
            key_valid = jnp.concatenate([jnp.ones((NV * BLK,), jnp.bool_), jnp.repeat(slash_valid, BLK)])
            key_pos = jnp.concatenate([vert_pos, slash_pos])
            allowed = key_valid[None, :] & (key_pos[None, :] <= query_pos[:, None])
            all_keys = jnp.concatenate([vert_keys, slash_keys]).astype(jnp.float32)
            all_values = jnp.concatenate([vert_values, slash_values]).astype(jnp.float32)
            scores = jnp.einsum('rhd,kd->hrk', query_rows.astype(jnp.float32), all_keys) * score_scale
            scores = jnp.where(allowed[None], scores, -1e+30)
            row_max = lax.optimization_barrier(jnp.max(scores, axis=2, keepdims=True))
            weights = jnp.exp(scores - row_max)
            denominator = lax.optimization_barrier(jnp.sum(weights, axis=2))
            rounded = lax.optimization_barrier(weights.astype(jnp.bfloat16)).astype(jnp.float32)
            weighted = jnp.einsum('hrk,kd->rhd', rounded, all_values)
            return (weighted / denominator.T[:, :, None]).astype(jnp.bfloat16)
        return lax.map(attend_block, jnp.arange(block_count).astype(jnp.int32))
    heads_out = lax.map(attend_head, jnp.arange(KVH).astype(jnp.int32))
    return jnp.transpose(heads_out, (1, 2, 0, 3, 4)).reshape(TOKENS, KVH * group_heads * HD)
```

```python
import functools
import math

import jax
import jax.numpy as jnp
from jax import lax
from jax.experimental import pallas as pl
from jax.experimental.pallas import tpu as pltpu
from jax.sharding import PartitionSpec as P

HD = 128
BLK = 64
LOOK = 2
NX = 4
NEG = -1e30
MESH = pl.DeviceIdType.MESH
F32 = jnp.float32
BF16 = jnp.bfloat16


def kernel(cfg, vert, slash, q_ref, k_ref, v_ref, out_ref, win_k, win_v, land1, land2, ext, rx, sx, rz, vall, bias, stage,
           own_send, own_recv, fwd_send, fwd_recv, xs_send, xs_recv, zs_send, zs_recv, zg_send, zg_recv, xg_send, xg_recv,
           out_send, out_recv, loc_sem):
    nx, nz, nh, nv, ns, nb, hq = cfg
    nctx = nx * nz
    bpc = nb // nh
    per = nv // nx
    vk = nv * BLK
    sk = ns * BLK
    ctx = lax.axis_index("ctx")
    me = lax.axis_index("head")
    x = ctx // nz
    z = ctx % nz
    nxt = (ctx + 1) % nctx
    prv = (ctx + nctx - 1) % nctx

    def xpeer(d):
        return ((x + d) % nx) * nz + z

    def zpeer(d):
        return x * nz + (z + d) % nz

    barrier = pltpu.get_barrier_semaphore()

    def greet(c, h):
        pl.semaphore_signal(barrier, inc=1, device_id={"ctx": c, "head": h}, device_id_type=MESH)

    greet(nxt, me)
    greet(prv, me)
    for d in range(1, nx):
        greet(xpeer(d), me)
    for d in range(1, nz):
        greet(zpeer(d), me)
    for d in range(1, nh):
        greet(ctx, (me + d) % nh)
    pl.semaphore_wait(barrier, 2 + (nx - 1) + (nz - 1) + (nh - 1))

    def remote(src, dst, ssem, rsem, c, h):
        return pltpu.make_async_remote_copy(src_ref=src, dst_ref=dst, send_sem=ssem, recv_sem=rsem,
                                            device_id={"ctx": c, "head": h}, device_id_type=MESH)

    def own_copy(k, part):
        ref = k_ref if part == 0 else v_ref
        return remote(ref.at[pl.ds(k * bpc, bpc)], land1.at[k, part], own_send.at[k, part],
                      own_recv.at[k, part], nxt, me)

    def fwd_copy(k):
        return remote(land1.at[k], land2.at[k], fwd_send.at[k], fwd_recv.at[k], nxt, me)

    def send_own(k):
        own_copy(k, 0).start()
        own_copy(k, 1).start()

    def take_own(k):
        own_copy(k, 0).wait_recv()
        own_copy(k, 1).wait_recv()
        fwd_copy(k).start()
        for b in range(bpc):
            win_k[nb + k * bpc + b] = land1[k, 0, b]
            win_v[nb + k * bpc + b] = land1[k, 1, b]

    own_left = [nh - 1 - k for k in range(nh)]
    take_left = list(own_left)

    def send_some(count):
        for _ in range(min(count, len(own_left))):
            send_own(own_left.pop(0))

    def take_some(count):
        for _ in range(min(count, len(take_left))):
            take_own(take_left.pop(0))

    send_some(3)

    for part in range(nx):
        for slot in range(per):
            rel = vert[0, part * per + slot] - ctx * nb
            mine = (rel >= 0) & (rel < nb)
            at = jnp.minimum(jnp.maximum(rel, 0), nb - 1)
            ext[part, slot] = jnp.where(mine, k_ref[at], jnp.zeros((BLK, HD), BF16))
            ext[part, per + slot] = jnp.where(mine, v_ref[at], jnp.zeros((BLK, HD), BF16))

    def xs_copy(d):
        return remote(ext.at[(x + d) % nx], rx.at[d - 1], xs_send.at[d - 1], xs_recv.at[d - 1], xpeer(d), me)

    def zs_copy(d):
        return remote(sx.at[(z + d) % nz], rz.at[d - 1], zs_send.at[d - 1], zs_recv.at[d - 1], zpeer(d), me)

    def zg_copy(d):
        return remote(vall.at[x, z], vall.at[x, z], zg_send.at[d - 1], zg_recv.at[d - 1], zpeer(d), me)

    def zg_arrival(d):
        src = (z + nz - d) % nz
        return remote(vall.at[x, src], vall.at[x, src], zg_send.at[d - 1], zg_recv.at[d - 1], zpeer(d), me)

    def xg_copy(d):
        return remote(vall.at[x], vall.at[x], xg_send.at[d - 1], xg_recv.at[d - 1], xpeer(d), me)

    def xg_arrival(d):
        src = (x + nx - d) % nx
        return remote(vall.at[src], vall.at[src], xg_send.at[d - 1], xg_recv.at[d - 1], xpeer(d), me)

    for d in range(1, nx):
        xs_copy(d).start()

    def copy_own(b, carry):
        win_k[LOOK * nb + b] = k_ref[b]
        win_v[LOOK * nb + b] = v_ref[b]
        return carry

    lax.fori_loop(0, nb, copy_own, 0)
    block = ctx * nb + lax.broadcasted_iota(jnp.int32, (nb, vk), 0)
    lane = lax.broadcasted_iota(jnp.int32, (nb, vk), 1) // BLK
    listed = jnp.zeros((nb, vk), jnp.int32)
    for n in range(nv):
        listed = jnp.where(lane == n, vert[0, n], listed)
    bias[:, 0:vk] = jnp.where(listed < block, 0.0, NEG)

    def offset(n):
        first = slash[0, 0]
        own = slash[0, n]
        return jnp.int32(0) if n == 0 else jnp.where(own == 0, first, own)

    reach = jnp.zeros((nb, sk), jnp.int32)
    for n in range(ns):
        reach = jnp.where(lane[:, 0:sk] == n, offset(n), reach)
    target = block[:, 0:sk] - reach
    good = target >= 0
    for n in range(nv):
        good = good & (target != vert[0, n])
    good = good | (lane[:, 0:sk] == 0)
    bias[:, vk:vk + sk] = jnp.where(good, 0.0, NEG)

    for d in range(1, nx):
        xs_copy(d).wait_recv()
    sx[...] = ext[x]
    for d in range(1, nx):
        sx[...] = sx[...] + rx[d - 1]
    for d in range(1, nz):
        zs_copy(d).start()
    send_some(2)
    take_some(1)
    for d in range(1, nz):
        zs_copy(d).wait_recv()
    piece = sx[z]
    for d in range(1, nz):
        piece = piece + rz[d - 1]
    vall[x, z] = piece
    for d in range(1, nz):
        zg_copy(d).start()
    send_some(2)
    take_some(2)
    for d in range(1, nz):
        zg_arrival(d).wait_recv()
    for d in range(1, nx):
        xg_copy(d).start()
    send_some(nh)
    take_some(nh)
    for d in range(1, nx):
        xg_arrival(d).wait_recv()

    factor = math.log2(math.e) / math.sqrt(HD)
    nt = (((1,), (1,)), ((), ()))
    cols = hq * HD
    qrows = hq * BLK
    tri_t = lax.broadcasted_iota(jnp.int32, (qrows, 2 * BLK), 0) % BLK
    tri_u = lax.broadcasted_iota(jnp.int32, (qrows, 2 * BLK), 1)
    causal = jnp.where((tri_u > tri_t) & (tri_u < BLK), NEG, 0.0)
    group = 256 // BLK

    def attend(r, to):
        q = q_ref[pl.ds(pl.multiple_of(r * BLK, BLK), BLK), :]
        qs = jnp.concatenate([q[:, h * HD:(h + 1) * HD] for h in range(hq)], axis=0)
        scores = []
        vals = []
        for part in range(nx):
            kk = vall[part, 0:per].reshape(per * BLK, HD)
            s = lax.dot_general(qs, kk, nt, preferred_element_type=F32)
            scores.append(s + bias[pl.ds(r, 1), part * per * BLK:(part + 1) * per * BLK])
            vals.append(lambda part=part: vall[part, per:2 * per].reshape(per * BLK, HD))
        for g in range(0, ns, group):
            at = [r + LOOK * nb - offset(n) for n in range(g, g + group)]
            kk = jnp.concatenate([win_k[a] for a in at], axis=0)
            s = lax.dot_general(qs, kk, nt, preferred_element_type=F32)
            s = s + bias[pl.ds(r, 1), vk + g * BLK:vk + (g + group) * BLK]
            if g == 0:
                s = jnp.concatenate([s[:, 0:2 * BLK] + causal, s[:, 2 * BLK:]], axis=1)
            scores.append(s)
            vals.append(lambda at=at: jnp.concatenate([win_v[a] for a in at], axis=0))
        top = jnp.max(scores[0], axis=1, keepdims=True)
        for s in scores[1:]:
            top = jnp.maximum(top, jnp.max(s, axis=1, keepdims=True))
        top = top * factor
        total = jnp.zeros((qrows, 1), F32)
        acc = jnp.zeros((qrows, HD), F32)
        for s, val in zip(scores, vals):
            w = jnp.exp2(s * factor - top)
            total = total + jnp.sum(w, axis=1, keepdims=True)
            acc = acc + jnp.dot(w.astype(BF16), val(), preferred_element_type=F32)
        o = (acc / total).astype(BF16)
        for h in range(hq):
            stage[to, pl.ds(pl.multiple_of((r % bpc) * BLK, BLK), BLK), h * HD:(h + 1) * HD] = o[h * BLK:(h + 1) * BLK]

    def out_copy(ch):
        return remote(stage.at[ch], out_ref.at[:, pl.ds(pl.multiple_of(me * cols, cols), cols)], out_send.at[ch],
                      out_recv.at[me], ctx, ch)

    def out_arrival(src):
        return remote(stage.at[src], out_ref.at[:, pl.ds(pl.multiple_of(src * cols, cols), cols)], out_send.at[src],
                      out_recv.at[src], ctx, src)

    def out_local():
        return pltpu.make_async_copy(stage.at[me], out_ref.at[:, pl.ds(pl.multiple_of(me * cols, cols), cols)], loc_sem)

    def chunk(step, carry):
        ch = nh - 1 - step
        fwd_copy(ch).wait_recv()

        def fill(b, c):
            win_k[ch * bpc + b] = land2[ch, 0, b]
            win_v[ch * bpc + b] = land2[ch, 1, b]
            return c

        lax.fori_loop(0, bpc, fill, 0)

        def one(j, c):
            attend(ch * bpc + bpc - 1 - j, ch)
            return c

        lax.fori_loop(0, bpc, one, 0)

        @pl.when(ch != me)
        def _():
            out_copy(ch).start()

        @pl.when(ch == me)
        def _():
            out_local().start()

        return carry

    lax.fori_loop(0, nh, chunk, 0)

    for k in range(nh):
        own_copy(k, 0).wait_send()
        own_copy(k, 1).wait_send()
        fwd_copy(k).wait_send()
    for d in range(1, nx):
        xs_copy(d).wait_send()
        xg_copy(d).wait_send()
    for d in range(1, nz):
        zs_copy(d).wait_send()
        zg_copy(d).wait_send()
    for ch in range(nh):
        @pl.when(ch != me)
        def _(ch=ch):
            out_copy(ch).wait_send()
            out_arrival(ch).wait_recv()
    out_local().wait()


def solution(mesh, nx=NX):
    nh = mesh.shape["head"]
    nctx = mesh.shape["ctx"]
    nz = nctx // nx

    def local(queries, keys, values, vertical, slash):
        tok, qcols = queries.shape
        hq = qcols // HD
        nb = tok // BLK
        nv = vertical.shape[1]
        ns = slash.shape[1]
        assert 2 * nv == nx * nz
        cfg = (nx, nz, nh, nv, ns, nb, hq)
        rows = tok // nh
        per = nv // nx
        dma = pltpu.SemaphoreType.DMA
        vmem = pl.BlockSpec(memory_space=pltpu.VMEM)
        smem = pl.BlockSpec(memory_space=pltpu.SMEM)
        return pl.pallas_call(
            functools.partial(kernel, cfg),
            out_shape=jax.ShapeDtypeStruct((rows, nh * qcols), BF16),
            in_specs=[smem, smem, vmem, vmem, vmem],
            out_specs=pl.BlockSpec(memory_space=pl.ANY),
            scratch_shapes=[
                pltpu.VMEM(((LOOK + 1) * nb, BLK, HD), BF16),
                pltpu.VMEM(((LOOK + 1) * nb, BLK, HD), BF16),
                pltpu.VMEM((nh, 2, nb // nh, BLK, HD), BF16),
                pltpu.VMEM((nh, 2, nb // nh, BLK, HD), BF16),
                pltpu.VMEM((nx, nz, BLK, HD), BF16),
                pltpu.VMEM((nx - 1, nz, BLK, HD), BF16),
                pltpu.VMEM((nz, BLK, HD), BF16),
                pltpu.VMEM((nz - 1, BLK, HD), BF16),
                pltpu.VMEM((nx, nz, BLK, HD), BF16),
                pltpu.VMEM((nb, (nv + ns) * BLK), F32),
                pltpu.VMEM((nh, rows, qcols), BF16),
                dma((nh, 2)), dma((nh, 2)), dma((nh,)), dma((nh,)),
                dma((nx - 1,)), dma((nx - 1,)), dma((nz - 1,)), dma((nz - 1,)),
                dma((nz - 1,)), dma((nz - 1,)), dma((nx - 1,)), dma((nx - 1,)),
                dma((nh,)), dma((nh,)), dma(()),
            ],
            compiler_params=pltpu.CompilerParams(collective_id=0, has_side_effects=True, vmem_limit_bytes=56 * 1024 * 1024),
        )(vertical, slash, queries, keys.reshape(nb, BLK, HD), values.reshape(nb, BLK, HD))

    in_specs = (P("ctx", "head"), P("ctx", "head"), P("ctx", "head"), P("head", None), P("head", None))
    return jax.shard_map(local, mesh=mesh, in_specs=in_specs, out_specs=P(("ctx", "head"), None), check_vma=False)
```

```python
import functools
import math

import jax
import jax.numpy as jnp
from jax import lax
from jax.experimental import pallas as pl
from jax.experimental.pallas import tpu as pltpu
from jax.sharding import PartitionSpec as P

HD = 128
BLK = 64
LOOK = 2
NX = 4
NEG = -1e30
MESH = pl.DeviceIdType.MESH
F32 = jnp.float32
BF16 = jnp.bfloat16


def kernel(cfg, vert, slash, q_ref, k_ref, v_ref, out_ref, q_buf, v_buf, win_k, win_v, land1, land2, land_a, ext, rx, sx, rz,
           vall, vturn, stage, buf_a, buf_b, tops, shifts, own_send, own_recv, fwd_send, fwd_recv, a_send, a_recv, bc_send, bc_recv, xs_send, xs_recv,
           zs_send, zs_recv, zg_send, zg_recv, xg_send, xg_recv, out_send, out_recv, loc_sem):
    nx, nz, nh, nv, ns, nb, hq = cfg
    nctx = nx * nz
    bpc = nb // nh
    per = nv // nx
    half = (nz - 2) // 2
    own0 = LOOK * nb
    cols = hq * HD
    qrows = hq * BLK
    group = 256 // BLK
    ctx = lax.axis_index("ctx")
    me = lax.axis_index("head")
    x = ctx // nz
    z = ctx % nz
    nxt = (ctx + 1) % nctx
    prv = (ctx + nctx - 1) % nctx

    def xpeer(d):
        return ((x + d) % nx) * nz + z

    def zpeer(d):
        return x * nz + (z + d) % nz

    relay_to = (zpeer(half) + 2) % nctx
    two_back = (ctx + nctx - 2) % nctx
    relay_from = (two_back // nz) * nz + (two_back % nz + nz - half) % nz

    load_k = pltpu.make_async_copy(k_ref, win_k.at[pl.ds(own0, nb)], loc_sem.at[0])
    load_v = pltpu.make_async_copy(v_ref, v_buf, loc_sem.at[1])
    load_q = pltpu.make_async_copy(q_ref, q_buf, loc_sem.at[2])
    load_k.start()
    load_v.start()
    load_q.start()

    barrier = pltpu.get_barrier_semaphore()

    def greet(c, h):
        pl.semaphore_signal(barrier, inc=1, device_id={"ctx": c, "head": h}, device_id_type=MESH)

    for c in (nxt, prv, relay_to, relay_from):
        greet(c, me)
    for d in range(1, nx):
        greet(xpeer(d), me)
    for d in range(1, nz):
        greet(zpeer(d), me)
    for d in range(1, nh):
        greet(ctx, (me + d) % nh)
    pl.semaphore_wait(barrier, 4 + (nx - 1) + (nz - 1) + (nh - 1))

    def remote(src, dst, ssem, rsem, c, h):
        return pltpu.make_async_remote_copy(src_ref=src, dst_ref=dst, send_sem=ssem, recv_sem=rsem,
                                            device_id={"ctx": c, "head": h}, device_id_type=MESH)

    def own_copy(k, part):
        ref = k_ref if part == 0 else v_ref
        return remote(ref.at[pl.ds(k * bpc, bpc)], land1.at[k, part], own_send.at[k, part], own_recv.at[k, part], nxt, me)

    def fwd_copy(k):
        return remote(land1.at[k], land2.at[k], fwd_send.at[k], fwd_recv.at[k], nxt, me)

    def a_copy(part):
        ref = k_ref if part == 0 else v_ref
        return remote(ref.at[pl.ds(0, bpc)], land_a.at[part], a_send.at[part], a_recv.at[part], zpeer(nz - half), me)

    def b_copy():
        return remote(land_a, land2.at[0], bc_send.at[0], bc_recv.at[0], relay_to, me)

    def c_copy():
        return remote(land2.at[0], land1.at[0], bc_send.at[1], bc_recv.at[1], prv, me)

    def send_own(k):
        own_copy(k, 0).start()
        own_copy(k, 1).start()

    def turn(dst, at, one, two):
        dst[at] = jnp.concatenate([one, two], axis=0).T
        dst[at + 1] = jnp.concatenate([two, one], axis=0).T

    def place(land, k, base):
        def pair(p, c):
            b = 2 * p
            at = base + k * bpc + b
            win_k[at] = land[k, 0, b]
            win_k[at + 1] = land[k, 0, b + 1]
            turn(win_v, at, land[k, 1, b], land[k, 1, b + 1])
            return c

        lax.fori_loop(0, bpc // 2, pair, 0)

    order = [nh - 1 - k for k in range(nh - 1)]
    a_copy(0).start()
    a_copy(1).start()
    for k in order[:4]:
        send_own(k)

    load_k.wait()
    load_v.wait()
    for part in range(nx):
        for slot in range(per):
            rel = vert[0, part * per + slot] - ctx * nb
            mine = (rel >= 0) & (rel < nb)
            at = jnp.minimum(jnp.maximum(rel, 0), nb - 1)
            ext[part, slot] = jnp.where(mine, win_k[own0 + at], jnp.zeros((BLK, HD), BF16))
            ext[part, per + slot] = jnp.where(mine, v_buf[at], jnp.zeros((BLK, HD), BF16))

    def xs_copy(d):
        return remote(ext.at[(x + d) % nx], rx.at[d - 1], xs_send.at[d - 1], xs_recv.at[d - 1], xpeer(d), me)

    def zs_copy(d):
        return remote(sx.at[(z + d) % nz], rz.at[d - 1], zs_send.at[d - 1], zs_recv.at[d - 1], zpeer(d), me)

    def zg_copy(d, src):
        return remote(vall.at[x, src], vall.at[x, src], zg_send.at[d - 1], zg_recv.at[d - 1], zpeer(d), me)

    def xg_copy(d, row, p):
        return remote(vall.at[row, p], vall.at[row, p], xg_send.at[d - 1, p], xg_recv.at[d - 1, p], xpeer(d), me)

    for d in range(1, nx):
        xs_copy(d).start()

    def own_turn(p, c):
        turn(win_v, own0 + 2 * p, v_buf[2 * p], v_buf[2 * p + 1])
        return c

    lax.fori_loop(0, nb // 2, own_turn, 0)

    for d in range(1, nx):
        xs_copy(d).wait_recv()
    sx[...] = ext[x]
    for d in range(1, nx):
        sx[...] = sx[...] + rx[d - 1]
    for d in range(1, nz):
        zs_copy(d).start()
    for k in order[4:6]:
        send_own(k)
    a_copy(0).wait_recv()
    a_copy(1).wait_recv()
    b_copy().start()
    for d in range(1, nz):
        zs_copy(d).wait_recv()
    piece = sx[z]
    for d in range(1, nz):
        piece = piece + rz[d - 1]
    vall[x, z] = piece
    for d in range(1, nz):
        zg_copy(d, z).start()
    for d in range(1, nx):
        xg_copy(d, x, z).start()
    for k in order[6:]:
        send_own(k)

    def take(j, c):
        k = nh - 1 - j
        own_copy(k, 0).wait_recv()
        own_copy(k, 1).wait_recv()
        fwd_copy(k).start()
        place(land1, k, nb)
        return c

    early = min(2, nh - 1)
    lax.fori_loop(0, early, take, 0)
    for d in range(1, nz):
        src = (z + nz - d) % nz
        zg_copy(d, src).wait_recv()
        for e in range(1, nx):
            xg_copy(e, x, src).start()
    b_copy().wait_recv()
    c_copy().start()
    lax.fori_loop(early, nh - 1, take, 0)

    for d in range(1, nx):
        row = (x + nx - d) % nx
        for p in range(nz):
            xg_copy(d, row, p).wait_recv()
    for part in range(nx):
        vturn[part] = vall[part, per:2 * per].reshape(per * BLK, HD).T
    load_q.wait()
    c_copy().wait_recv()
    place(land1, 0, nb)

    factor = math.log2(math.e) / math.sqrt(HD)
    nt = (((1,), (1,)), ((), ()))
    key_at = lax.broadcasted_iota(jnp.int32, (BLK, qrows), 0)
    row_at = lax.broadcasted_iota(jnp.int32, (BLK, qrows), 1) % BLK
    lanes = lax.broadcasted_iota(jnp.int32, (HD, 2 * BLK), 1)
    low = jnp.where(lanes < BLK, 1.0, 0.0).astype(BF16)
    high = jnp.where(lanes < BLK, 0.0, 1.0).astype(BF16)

    def offset(n):
        first = slash[0, 0]
        own = slash[0, n]
        return jnp.int32(0) if n == 0 else jnp.where(own == 0, first, own)

    tiles = [(g, per) for g in range(nx)] + [(nx + g, group) for g in range(ns // group)]
    starts = [sum(w for _, w in tiles[:t]) for t in range(len(tiles))]

    def scorer(r, buf, slot):
        q = q_buf[pl.ds(pl.multiple_of(r * BLK, BLK), BLK), :]
        qs = jnp.concatenate([q[:, h * HD:(h + 1) * HD] for h in range(hq)], axis=0)
        i = ctx * nb + r
        state = [jnp.full((8, qrows), NEG, F32)]

        def tile(t):
            g, width = tiles[t]
            if g < nx:
                kk = vall[g, 0:per].reshape(per * BLK, HD)
            else:
                kk = jnp.concatenate([win_k[r + own0 - offset((g - nx) * group + n)] for n in range(group)], axis=0)
            s = lax.dot_general(kk, qs, nt, preferred_element_type=F32)
            for n in range(width):
                at = starts[t] + n
                block = s[n * BLK:(n + 1) * BLK]
                if g < nx:
                    shift = jnp.where(vert[0, at] < i, 0.0, NEG)
                elif at == nv:
                    block = jnp.where(key_at > row_at, NEG, block)
                    shift = jnp.float32(0.0)
                else:
                    target = i - offset(at - nv)
                    bad = target < 0
                    for m in range(nv):
                        bad = bad | (target == vert[0, m])
                    shift = jnp.where(bad, NEG, 0.0)
                shifts[slot, at] = shift
                buf[at * BLK:(at + 1) * BLK, :] = block
                state[0] = jnp.maximum(state[0], jnp.max(block.reshape(BLK // 8, 8, qrows), axis=0) + shift)

        def done():
            tops[slot] = jnp.broadcast_to(jnp.max(state[0], axis=0, keepdims=True) * factor, (8, qrows))

        return tile, done

    def weigher(r, buf, slot):
        top = tops[slot, 0:1]
        state = [jnp.zeros((8, qrows), F32), jnp.zeros((HD, qrows), F32)]

        def tile(t):
            g, width = tiles[t]
            ws = []
            for n in range(width):
                at = starts[t] + n
                w = jnp.exp2(buf[at * BLK:(at + 1) * BLK, :] * factor - (top - shifts[slot, at]))
                state[0] = state[0] + jnp.sum(w.reshape(BLK // 8, 8, qrows), axis=0)
                ws.append(w.astype(BF16))
            w = jnp.concatenate(ws, axis=0)
            if g < nx:
                vt = vturn[g]
            else:
                pairs = []
                for n in range(0, group, 2):
                    one = r + own0 - offset((g - nx) * group + n)
                    two = r + own0 - offset((g - nx) * group + n + 1)
                    pairs.append(win_v[one] * low + win_v[two ^ 1] * high)
                vt = jnp.concatenate(pairs, axis=1)
            state[1] = state[1] + jnp.dot(vt, w, preferred_element_type=F32)

        def done():
            o = (state[1] / jnp.sum(state[0], axis=0, keepdims=True)).T.astype(BF16)
            for h in range(hq):
                stage[r // bpc, pl.ds(pl.multiple_of((r % bpc) * BLK, BLK), BLK), h * HD:(h + 1) * HD] = o[h * BLK:(h + 1) * BLK]

        return tile, done

    def both(r_next, buf_next, slot_next, r, buf, slot):
        score, score_done = scorer(r_next, buf_next, slot_next)
        weigh, weigh_done = weigher(r, buf, slot)
        for t in range(len(tiles)):
            score(t)
            weigh(t)
        score_done()
        weigh_done()

    def out_copy(ch):
        return remote(stage.at[ch], out_ref.at[:, pl.ds(pl.multiple_of(me * cols, cols), cols)], out_send.at[ch],
                      out_recv.at[me], ctx, ch)

    def out_arrival(src):
        return remote(stage.at[src], out_ref.at[:, pl.ds(pl.multiple_of(src * cols, cols), cols)], out_send.at[src],
                      out_recv.at[src], ctx, src)

    def out_local():
        return pltpu.make_async_copy(stage.at[me], out_ref.at[:, pl.ds(pl.multiple_of(me * cols, cols), cols)], loc_sem.at[3])

    last = nb - 1
    fwd_copy(nh - 1).wait_recv()
    place(land2, nh - 1, 0)
    score, score_done = scorer(last, buf_a, 0)
    for t in range(len(tiles)):
        score(t)
    score_done()

    def two_blocks(u, carry):
        odd = last - 2 * u
        both(odd - 1, buf_b, 1, odd, buf_a, 0)
        even = odd - 1
        ch = even // bpc
        ends = even % bpc == 0

        @pl.when(ends & (ch > 1))
        def _():
            fwd_copy(ch - 1).wait_recv()

        @pl.when(ends & (ch > 0))
        def _():
            place(land2, ch - 1, 0)

        both(jnp.maximum(even - 1, 0), buf_a, 0, even, buf_b, 1)

        @pl.when(ends & (ch != me))
        def _():
            out_copy(ch).start()

        @pl.when(ends & (ch == me))
        def _():
            out_local().start()

        return carry

    lax.fori_loop(0, nb // 2, two_blocks, 0)

    for k in range(1, nh):
        own_copy(k, 0).wait_send()
        own_copy(k, 1).wait_send()
        fwd_copy(k).wait_send()
    a_copy(0).wait_send()
    a_copy(1).wait_send()
    b_copy().wait_send()
    c_copy().wait_send()
    for d in range(1, nx):
        xs_copy(d).wait_send()
        for p in range(nz):
            xg_copy(d, x, p).wait_send()
    for d in range(1, nz):
        zs_copy(d).wait_send()
        zg_copy(d, z).wait_send()
    for ch in range(nh):
        @pl.when(ch != me)
        def _(ch=ch):
            out_copy(ch).wait_send()
            out_arrival(ch).wait_recv()
    out_local().wait()


def solution(mesh, nx=NX):
    nh = mesh.shape["head"]
    nctx = mesh.shape["ctx"]
    nz = nctx // nx

    def local(queries, keys, values, vertical, slash):
        tok, qcols = queries.shape
        hq = qcols // HD
        nb = tok // BLK
        nv = vertical.shape[1]
        ns = slash.shape[1]
        assert 2 * nv == nx * nz
        cfg = (nx, nz, nh, nv, ns, nb, hq)
        rows = tok // nh
        per = nv // nx
        dma = pltpu.SemaphoreType.DMA
        hbm = pl.BlockSpec(memory_space=pl.ANY)
        smem = pl.BlockSpec(memory_space=pltpu.SMEM)
        return pl.pallas_call(
            functools.partial(kernel, cfg),
            out_shape=jax.ShapeDtypeStruct((rows, nh * qcols), BF16),
            in_specs=[smem, smem, hbm, hbm, hbm],
            out_specs=hbm,
            scratch_shapes=[
                pltpu.VMEM((tok, qcols), BF16),
                pltpu.VMEM((nb, BLK, HD), BF16),
                pltpu.VMEM(((LOOK + 1) * nb, BLK, HD), BF16),
                pltpu.VMEM(((LOOK + 1) * nb, HD, 2 * BLK), BF16),
                pltpu.VMEM((nh, 2, nb // nh, BLK, HD), BF16),
                pltpu.VMEM((nh, 2, nb // nh, BLK, HD), BF16),
                pltpu.VMEM((2, nb // nh, BLK, HD), BF16),
                pltpu.VMEM((nx, nz, BLK, HD), BF16),
                pltpu.VMEM((nx - 1, nz, BLK, HD), BF16),
                pltpu.VMEM((nz, BLK, HD), BF16),
                pltpu.VMEM((nz - 1, BLK, HD), BF16),
                pltpu.VMEM((nx, nz, BLK, HD), BF16),
                pltpu.VMEM((nx, HD, per * BLK), BF16),
                pltpu.VMEM((nh, rows, qcols), BF16),
                pltpu.VMEM(((nv + ns) * BLK, hq * BLK), F32),
                pltpu.VMEM(((nv + ns) * BLK, hq * BLK), F32),
                pltpu.VMEM((2, 8, hq * BLK), F32),
                pltpu.SMEM((2, nv + ns), F32),
                dma((nh, 2)), dma((nh, 2)), dma((nh,)), dma((nh,)), dma((2,)), dma((2,)), dma((2,)), dma((2,)),
                dma((nx - 1,)), dma((nx - 1,)), dma((nz - 1,)), dma((nz - 1,)),
                dma((nz - 1,)), dma((nz - 1,)), dma((nx - 1, nz)), dma((nx - 1, nz)),
                dma((nh,)), dma((nh,)), dma((4,)),
            ],
            compiler_params=pltpu.CompilerParams(collective_id=0, has_side_effects=True, vmem_limit_bytes=56 * 1024 * 1024),
        )(vertical, slash, queries, keys.reshape(nb, BLK, HD), values.reshape(nb, BLK, HD))

    in_specs = (P("ctx", "head"), P("ctx", "head"), P("ctx", "head"), P("head", None), P("head", None))
    return jax.shard_map(local, mesh=mesh, in_specs=in_specs, out_specs=P(("ctx", "head"), None), check_vma=False)
```

```python
import functools
import math

import jax
import jax.numpy as jnp
from jax import lax
from jax.experimental import pallas as pl
from jax.experimental.pallas import tpu as pltpu
from jax.sharding import PartitionSpec as P

HD = 128
BLK = 64
LOOK = 2
NX = 4
NEG = -1e30
MESH = pl.DeviceIdType.MESH
F32 = jnp.float32
BF16 = jnp.bfloat16


def kernel(cfg, vert, slash, q_ref, k_ref, v_ref, out_ref, q_buf, v_buf, win_k, win_v, land1, land2, land_a, land_r, ext, rx, sx, rz,
           vall, vturn, stage, buf_a, buf_b, tops, shifts, own_send, own_recv, fwd_send, fwd_recv, a_send, a_recv, bc_send, bc_recv, r_send, r_recv, xs_send, xs_recv,
           zs_send, zs_recv, zg_send, zg_recv, xg_send, xg_recv, out_send, out_recv, loc_sem):
    nx, nz, nh, nv, ns, nb, hq = cfg
    nctx = nx * nz
    bpc = nb // nh
    per = nv // nx
    half = (nz - 2) // 2
    own0 = LOOK * nb
    cols = hq * HD
    qrows = hq * BLK
    group = 256 // BLK
    ctx = lax.axis_index("ctx")
    me = lax.axis_index("head")
    x = ctx // nz
    z = ctx % nz
    nxt = (ctx + 1) % nctx
    prv = (ctx + nctx - 1) % nctx

    def xpeer(d):
        return ((x + d) % nx) * nz + z

    def zpeer(d):
        return x * nz + (z + d) % nz

    relay_to = (zpeer(half) + 2) % nctx
    two_back = (ctx + nctx - 2) % nctx
    relay_from = (two_back // nz) * nz + (two_back % nz + nz - half) % nz

    load_k = pltpu.make_async_copy(k_ref, win_k.at[pl.ds(own0, nb)], loc_sem.at[0])
    load_v = pltpu.make_async_copy(v_ref, v_buf, loc_sem.at[1])
    load_q = pltpu.make_async_copy(q_ref, q_buf, loc_sem.at[2])
    load_k.start()
    load_v.start()
    load_q.start()

    barrier = pltpu.get_barrier_semaphore()

    def greet(c, h):
        pl.semaphore_signal(barrier, inc=1, device_id={"ctx": c, "head": h}, device_id_type=MESH)

    for c in (nxt, prv, relay_to, relay_from):
        greet(c, me)
    for d in range(1, nx):
        greet(xpeer(d), me)
    for d in range(1, nz):
        greet(zpeer(d), me)
    for d in range(1, nh):
        greet(ctx, (me + d) % nh)
    pl.semaphore_wait(barrier, 4 + (nx - 1) + (nz - 1) + (nh - 1))

    def remote(src, dst, ssem, rsem, c, h):
        return pltpu.make_async_remote_copy(src_ref=src, dst_ref=dst, send_sem=ssem, recv_sem=rsem,
                                            device_id={"ctx": c, "head": h}, device_id_type=MESH)

    def own_copy(k, part):
        ref = k_ref if part == 0 else v_ref
        return remote(ref.at[pl.ds(k * bpc, bpc)], land1.at[k, part], own_send.at[k, part], own_recv.at[k, part], nxt, me)

    def fwd_copy(k):
        return remote(land1.at[k], land2.at[k], fwd_send.at[k], fwd_recv.at[k], nxt, me)

    def turn_copy(k):
        return remote(land1.at[k], land_r.at[k], fwd_send.at[k], r_recv.at[k], xpeer(1), me)

    def relay_copy(k):
        return remote(land_r.at[k], land2.at[k], r_send.at[k], fwd_recv.at[k], x * nz, me)

    def relay(k):
        @pl.when(z == nz - 1)
        def _():
            turn_copy(k).wait_recv()
            relay_copy(k).start()

    def a_copy(part):
        ref = k_ref if part == 0 else v_ref
        return remote(ref.at[pl.ds(0, bpc)], land_a.at[part], a_send.at[part], a_recv.at[part], zpeer(nz - half), me)

    def b_copy():
        return remote(land_a, land2.at[0], bc_send.at[0], bc_recv.at[0], relay_to, me)

    def c_copy():
        return remote(land2.at[0], land1.at[0], bc_send.at[1], bc_recv.at[1], prv, me)

    def send_own(k):
        own_copy(k, 0).start()
        own_copy(k, 1).start()

    def turn(dst, at, one, two):
        dst[at] = jnp.concatenate([one, two], axis=0).T
        dst[at + 1] = jnp.concatenate([two, one], axis=0).T

    def place(land, k, base):
        def pair(p, c):
            b = 2 * p
            at = base + k * bpc + b
            win_k[at] = land[k, 0, b]
            win_k[at + 1] = land[k, 0, b + 1]
            turn(win_v, at, land[k, 1, b], land[k, 1, b + 1])
            return c

        lax.fori_loop(0, bpc // 2, pair, 0)

    order = [nh - 1 - k for k in range(nh - 1)]
    a_copy(0).start()
    a_copy(1).start()
    @pl.when(z != nz - 1)
    def _():
        for k in order[:4]:
            send_own(k)

    load_k.wait()
    load_v.wait()
    for part in range(nx):
        for slot in range(per):
            rel = vert[0, part * per + slot] - ctx * nb
            mine = (rel >= 0) & (rel < nb)
            at = jnp.minimum(jnp.maximum(rel, 0), nb - 1)
            ext[part, slot] = jnp.where(mine, win_k[own0 + at], jnp.zeros((BLK, HD), BF16))
            ext[part, per + slot] = jnp.where(mine, v_buf[at], jnp.zeros((BLK, HD), BF16))

    def xs_copy(d):
        return remote(ext.at[(x + d) % nx], rx.at[d - 1], xs_send.at[d - 1], xs_recv.at[d - 1], xpeer(d), me)

    def zs_copy(d):
        return remote(sx.at[(z + d) % nz], rz.at[d - 1], zs_send.at[d - 1], zs_recv.at[d - 1], zpeer(d), me)

    def zg_copy(d, src):
        return remote(vall.at[x, src], vall.at[x, src], zg_send.at[d - 1], zg_recv.at[d - 1], zpeer(d), me)

    def xg_copy(d, row, p):
        return remote(vall.at[row, p], vall.at[row, p], xg_send.at[d - 1, p], xg_recv.at[d - 1, p], xpeer(d), me)

    for d in range(1, nx):
        xs_copy(d).start()

    def own_turn(p, c):
        turn(win_v, own0 + 2 * p, v_buf[2 * p], v_buf[2 * p + 1])
        return c

    lax.fori_loop(0, nb // 2, own_turn, 0)

    for d in range(1, nx):
        xs_copy(d).wait_recv()
    sx[...] = ext[x]
    for d in range(1, nx):
        sx[...] = sx[...] + rx[d - 1]
    for d in range(1, nz):
        zs_copy(d).start()
    @pl.when(z == nz - 1)
    def _():
        for k in order[:4]:
            send_own(k)

    for k in order[4:6]:
        send_own(k)
    a_copy(0).wait_recv()
    a_copy(1).wait_recv()
    b_copy().start()
    for d in range(1, nz):
        zs_copy(d).wait_recv()
    piece = sx[z]
    for d in range(1, nz):
        piece = piece + rz[d - 1]
    vall[x, z] = piece
    for d in range(1, nz):
        zg_copy(d, z).start()
    for d in range(1, nx):
        xg_copy(d, x, z).start()
    for k in order[6:]:
        send_own(k)

    def take(j, c):
        k = nh - 1 - j
        own_copy(k, 0).wait_recv()
        own_copy(k, 1).wait_recv()

        @pl.when(z != nz - 1)
        def _():
            fwd_copy(k).start()

        @pl.when(z == nz - 1)
        def _():
            turn_copy(k).start()

        place(land1, k, nb)

        @pl.when(j > 0)
        def _():
            relay(k + 1)

        return c

    early = min(2, nh - 1)
    lax.fori_loop(0, early, take, 0)
    for d in range(1, nz):
        src = (z + nz - d) % nz
        zg_copy(d, src).wait_recv()
        for e in range(1, nx):
            xg_copy(e, x, src).start()
    b_copy().wait_recv()
    c_copy().start()
    lax.fori_loop(early, nh - 1, take, 0)
    relay(1)

    for d in range(1, nx):
        row = (x + nx - d) % nx
        for p in range(nz):
            xg_copy(d, row, p).wait_recv()
    for part in range(nx):
        vturn[part] = vall[part, per:2 * per].reshape(per * BLK, HD).T
    load_q.wait()
    c_copy().wait_recv()
    place(land1, 0, nb)

    factor = math.log2(math.e) / math.sqrt(HD)
    nt = (((1,), (1,)), ((), ()))
    key_at = lax.broadcasted_iota(jnp.int32, (BLK, qrows), 0)
    row_at = lax.broadcasted_iota(jnp.int32, (BLK, qrows), 1) % BLK
    lanes = lax.broadcasted_iota(jnp.int32, (HD, 2 * BLK), 1)
    low = jnp.where(lanes < BLK, 1.0, 0.0).astype(BF16)
    high = jnp.where(lanes < BLK, 0.0, 1.0).astype(BF16)

    def offset(n):
        first = slash[0, 0]
        own = slash[0, n]
        return jnp.int32(0) if n == 0 else jnp.where(own == 0, first, own)

    tiles = [(g, per) for g in range(nx)] + [(nx + g, group) for g in range(ns // group)]
    starts = [sum(w for _, w in tiles[:t]) for t in range(len(tiles))]

    def scorer(r, buf, slot):
        q = q_buf[pl.ds(pl.multiple_of(r * BLK, BLK), BLK), :]
        qs = jnp.concatenate([q[:, h * HD:(h + 1) * HD] for h in range(hq)], axis=0)
        i = ctx * nb + r
        state = [jnp.full((8, qrows), NEG, F32)]

        def tile(t):
            g, width = tiles[t]
            if g < nx:
                kk = vall[g, 0:per].reshape(per * BLK, HD)
            else:
                kk = jnp.concatenate([win_k[r + own0 - offset((g - nx) * group + n)] for n in range(group)], axis=0)
            s = lax.dot_general(kk, qs, nt, preferred_element_type=F32)
            for n in range(width):
                at = starts[t] + n
                block = s[n * BLK:(n + 1) * BLK]
                if g < nx:
                    shift = jnp.where(vert[0, at] < i, 0.0, NEG)
                elif at == nv:
                    block = jnp.where(key_at > row_at, NEG, block)
                    shift = jnp.float32(0.0)
                else:
                    target = i - offset(at - nv)
                    bad = target < 0
                    for m in range(nv):
                        bad = bad | (target == vert[0, m])
                    shift = jnp.where(bad, NEG, 0.0)
                shifts[slot, at] = shift
                buf[at * BLK:(at + 1) * BLK, :] = block
                state[0] = jnp.maximum(state[0], jnp.max(block.reshape(BLK // 8, 8, qrows), axis=0) + shift)

        def done():
            tops[slot] = jnp.broadcast_to(jnp.max(state[0], axis=0, keepdims=True) * factor, (8, qrows))

        return tile, done

    def weigher(r, buf, slot):
        top = tops[slot, 0:1]
        state = [jnp.zeros((8, qrows), F32), jnp.zeros((HD, qrows), F32)]

        def tile(t):
            g, width = tiles[t]
            ws = []
            for n in range(width):
                at = starts[t] + n
                w = jnp.exp2(buf[at * BLK:(at + 1) * BLK, :] * factor - (top - shifts[slot, at]))
                state[0] = state[0] + jnp.sum(w.reshape(BLK // 8, 8, qrows), axis=0)
                ws.append(w.astype(BF16))
            w = jnp.concatenate(ws, axis=0)
            if g < nx:
                vt = vturn[g]
            else:
                pairs = []
                for n in range(0, group, 2):
                    one = r + own0 - offset((g - nx) * group + n)
                    two = r + own0 - offset((g - nx) * group + n + 1)
                    pairs.append(win_v[one] * low + win_v[two ^ 1] * high)
                vt = jnp.concatenate(pairs, axis=1)
            state[1] = state[1] + jnp.dot(vt, w, preferred_element_type=F32)

        def done():
            o = (state[1] / jnp.sum(state[0], axis=0, keepdims=True)).T.astype(BF16)
            for h in range(hq):
                stage[r // bpc, pl.ds(pl.multiple_of((r % bpc) * BLK, BLK), BLK), h * HD:(h + 1) * HD] = o[h * BLK:(h + 1) * BLK]

        return tile, done

    def both(r_next, buf_next, slot_next, r, buf, slot):
        score, score_done = scorer(r_next, buf_next, slot_next)
        weigh, weigh_done = weigher(r, buf, slot)
        for t in range(len(tiles)):
            score(t)
            weigh(t)
        score_done()
        weigh_done()

    def out_copy(ch):
        return remote(stage.at[ch], out_ref.at[:, pl.ds(pl.multiple_of(me * cols, cols), cols)], out_send.at[ch],
                      out_recv.at[me], ctx, ch)

    def out_arrival(src):
        return remote(stage.at[src], out_ref.at[:, pl.ds(pl.multiple_of(src * cols, cols), cols)], out_send.at[src],
                      out_recv.at[src], ctx, src)

    def out_local():
        return pltpu.make_async_copy(stage.at[me], out_ref.at[:, pl.ds(pl.multiple_of(me * cols, cols), cols)], loc_sem.at[3])

    last = nb - 1
    fwd_copy(nh - 1).wait_recv()
    place(land2, nh - 1, 0)
    score, score_done = scorer(last, buf_a, 0)
    for t in range(len(tiles)):
        score(t)
    score_done()

    def two_blocks(u, carry):
        odd = last - 2 * u
        both(odd - 1, buf_b, 1, odd, buf_a, 0)
        even = odd - 1
        ch = even // bpc
        ends = even % bpc == 0

        @pl.when(ends & (ch > 1))
        def _():
            fwd_copy(ch - 1).wait_recv()

        @pl.when(ends & (ch > 0))
        def _():
            place(land2, ch - 1, 0)

        both(jnp.maximum(even - 1, 0), buf_a, 0, even, buf_b, 1)

        @pl.when(ends & (ch != me))
        def _():
            out_copy(ch).start()

        @pl.when(ends & (ch == me))
        def _():
            out_local().start()

        return carry

    lax.fori_loop(0, nb // 2, two_blocks, 0)

    for k in range(1, nh):
        own_copy(k, 0).wait_send()
        own_copy(k, 1).wait_send()
        fwd_copy(k).wait_send()

        @pl.when(z == nz - 1)
        def _(k=k):
            relay_copy(k).wait_send()
    a_copy(0).wait_send()
    a_copy(1).wait_send()
    b_copy().wait_send()
    c_copy().wait_send()
    for d in range(1, nx):
        xs_copy(d).wait_send()
        for p in range(nz):
            xg_copy(d, x, p).wait_send()
    for d in range(1, nz):
        zs_copy(d).wait_send()
        zg_copy(d, z).wait_send()
    for ch in range(nh):
        @pl.when(ch != me)
        def _(ch=ch):
            out_copy(ch).wait_send()
            out_arrival(ch).wait_recv()
    out_local().wait()


def solution(mesh, nx=NX):
    nh = mesh.shape["head"]
    nctx = mesh.shape["ctx"]
    nz = nctx // nx

    def local(queries, keys, values, vertical, slash):
        tok, qcols = queries.shape
        hq = qcols // HD
        nb = tok // BLK
        nv = vertical.shape[1]
        ns = slash.shape[1]
        assert 2 * nv == nx * nz
        cfg = (nx, nz, nh, nv, ns, nb, hq)
        rows = tok // nh
        per = nv // nx
        dma = pltpu.SemaphoreType.DMA
        hbm = pl.BlockSpec(memory_space=pl.ANY)
        smem = pl.BlockSpec(memory_space=pltpu.SMEM)
        return pl.pallas_call(
            functools.partial(kernel, cfg),
            out_shape=jax.ShapeDtypeStruct((rows, nh * qcols), BF16),
            in_specs=[smem, smem, hbm, hbm, hbm],
            out_specs=hbm,
            scratch_shapes=[
                pltpu.VMEM((tok, qcols), BF16),
                pltpu.VMEM((nb, BLK, HD), BF16),
                pltpu.VMEM(((LOOK + 1) * nb, BLK, HD), BF16),
                pltpu.VMEM(((LOOK + 1) * nb, HD, 2 * BLK), BF16),
                pltpu.VMEM((nh, 2, nb // nh, BLK, HD), BF16),
                pltpu.VMEM((nh, 2, nb // nh, BLK, HD), BF16),
                pltpu.VMEM((2, nb // nh, BLK, HD), BF16),
                pltpu.VMEM((nh, 2, nb // nh, BLK, HD), BF16),
                pltpu.VMEM((nx, nz, BLK, HD), BF16),
                pltpu.VMEM((nx - 1, nz, BLK, HD), BF16),
                pltpu.VMEM((nz, BLK, HD), BF16),
                pltpu.VMEM((nz - 1, BLK, HD), BF16),
                pltpu.VMEM((nx, nz, BLK, HD), BF16),
                pltpu.VMEM((nx, HD, per * BLK), BF16),
                pltpu.VMEM((nh, rows, qcols), BF16),
                pltpu.VMEM(((nv + ns) * BLK, hq * BLK), F32),
                pltpu.VMEM(((nv + ns) * BLK, hq * BLK), F32),
                pltpu.VMEM((2, 8, hq * BLK), F32),
                pltpu.SMEM((2, nv + ns), F32),
                dma((nh, 2)), dma((nh, 2)), dma((nh,)), dma((nh,)), dma((2,)), dma((2,)), dma((2,)), dma((2,)), dma((nh,)), dma((nh,)),
                dma((nx - 1,)), dma((nx - 1,)), dma((nz - 1,)), dma((nz - 1,)),
                dma((nz - 1,)), dma((nz - 1,)), dma((nx - 1, nz)), dma((nx - 1, nz)),
                dma((nh,)), dma((nh,)), dma((4,)),
            ],
            compiler_params=pltpu.CompilerParams(collective_id=0, has_side_effects=True, vmem_limit_bytes=56 * 1024 * 1024),
        )(vertical, slash, queries, keys.reshape(nb, BLK, HD), values.reshape(nb, BLK, HD))

    in_specs = (P("ctx", "head"), P("ctx", "head"), P("ctx", "head"), P("head", None), P("head", None))
    return jax.shard_map(local, mesh=mesh, in_specs=in_specs, out_specs=P(("ctx", "head"), None), check_vma=False)
```

```python
import functools
import math

import jax
import jax.numpy as jnp
from jax import lax
from jax.experimental import pallas as pl
from jax.experimental.pallas import tpu as pltpu
from jax.sharding import PartitionSpec as P

HD = 128
BLK = 64
LOOK = 2
NX = 4
NEG = -1e30
MESH = pl.DeviceIdType.MESH
F32 = jnp.float32
BF16 = jnp.bfloat16


def kernel(cfg, vert, slash, q_ref, k_ref, v_ref, out_ref, q_buf, v_buf, win_k, win_v, land1, land2, land_a, land_r, ext, rx, sx, rz,
           vall, vturn, stage, buf_a, buf_b, tops, shifts, own_send, own_recv, fwd_send, fwd_recv, a_send, a_recv, bc_send, bc_recv, r_send, r_recv, xs_send, xs_recv,
           zs_send, zs_recv, zg_send, zg_recv, xg_send, xg_recv, out_send, out_recv, loc_sem):
    nx, nz, nh, nv, ns, nb, hq = cfg
    nctx = nx * nz
    bpc = nb // nh
    per = nv // nx
    half = (nz - 2) // 2
    own0 = LOOK * nb
    cols = hq * HD
    qrows = hq * BLK
    group = 256 // BLK
    ctx = lax.axis_index("ctx")
    me = lax.axis_index("head")
    x = ctx // nz
    z = ctx % nz
    nxt = (ctx + 1) % nctx
    prv = (ctx + nctx - 1) % nctx

    def xpeer(d):
        return ((x + d) % nx) * nz + z

    def zpeer(d):
        return x * nz + (z + d) % nz

    relay_to = (zpeer(half) + 2) % nctx
    two_back = (ctx + nctx - 2) % nctx
    relay_from = (two_back // nz) * nz + (two_back % nz + nz - half) % nz

    load_k = pltpu.make_async_copy(k_ref, win_k.at[pl.ds(own0, nb)], loc_sem.at[0])
    load_v = pltpu.make_async_copy(v_ref, v_buf, loc_sem.at[1])
    load_q = pltpu.make_async_copy(q_ref, q_buf, loc_sem.at[2])
    load_k.start()
    load_v.start()
    load_q.start()

    barrier = pltpu.get_barrier_semaphore()

    def greet(c, h):
        pl.semaphore_signal(barrier, inc=1, device_id={"ctx": c, "head": h}, device_id_type=MESH)

    for c in (nxt, prv, relay_to, relay_from):
        greet(c, me)
    for d in range(1, nx):
        greet(xpeer(d), me)
    for d in range(1, nz):
        greet(zpeer(d), me)
    for d in range(1, nh):
        greet(ctx, (me + d) % nh)
    pl.semaphore_wait(barrier, 4 + (nx - 1) + (nz - 1) + (nh - 1))

    def remote(src, dst, ssem, rsem, c, h):
        return pltpu.make_async_remote_copy(src_ref=src, dst_ref=dst, send_sem=ssem, recv_sem=rsem,
                                            device_id={"ctx": c, "head": h}, device_id_type=MESH)

    def own_copy(k, part):
        ref = k_ref if part == 0 else v_ref
        return remote(ref.at[pl.ds(k * bpc, bpc)], land1.at[k, part], own_send.at[k, part], own_recv.at[k, part], nxt, me)

    def fwd_copy(k):
        return remote(land1.at[k], land2.at[k], fwd_send.at[k], fwd_recv.at[k], nxt, me)

    def turn_copy(k):
        return remote(land1.at[k], land_r.at[k], fwd_send.at[k], r_recv.at[k], xpeer(1), me)

    def relay_copy(k):
        return remote(land_r.at[k], land2.at[k], r_send.at[k], fwd_recv.at[k], x * nz, me)

    def relay(k):
        @pl.when(z == nz - 1)
        def _():
            turn_copy(k).wait_recv()
            relay_copy(k).start()

    def a_copy(part):
        ref = k_ref if part == 0 else v_ref
        return remote(ref.at[pl.ds(0, bpc)], land_a.at[part], a_send.at[part], a_recv.at[part], zpeer(nz - half), me)

    def b_copy():
        return remote(land_a, land2.at[0], bc_send.at[0], bc_recv.at[0], relay_to, me)

    def c_copy():
        return remote(land2.at[0], land1.at[0], bc_send.at[1], bc_recv.at[1], prv, me)

    def send_own(k):
        own_copy(k, 0).start()
        own_copy(k, 1).start()

    def turn(dst, at, one, two):
        dst[at] = jnp.concatenate([one, two], axis=0).T
        dst[at + 1] = jnp.concatenate([two, one], axis=0).T

    def place(land, k, base):
        def pair(p, c):
            b = 2 * p
            at = base + k * bpc + b
            win_k[at] = land[k, 0, b]
            win_k[at + 1] = land[k, 0, b + 1]
            turn(win_v, at, land[k, 1, b], land[k, 1, b + 1])
            return c

        lax.fori_loop(0, bpc // 2, pair, 0)

    order = [nh - 1 - k for k in range(nh - 1)]
    a_copy(0).start()
    a_copy(1).start()
    @pl.when(z != nz - 1)
    def _():
        for k in order[:4]:
            send_own(k)

    load_k.wait()
    load_v.wait()
    for part in range(nx):
        for slot in range(per):
            rel = vert[0, part * per + slot] - ctx * nb
            mine = (rel >= 0) & (rel < nb)
            at = jnp.minimum(jnp.maximum(rel, 0), nb - 1)
            ext[part, slot] = jnp.where(mine, win_k[own0 + at], jnp.zeros((BLK, HD), BF16))
            ext[part, per + slot] = jnp.where(mine, v_buf[at], jnp.zeros((BLK, HD), BF16))

    def xs_copy(d):
        return remote(ext.at[(x + d) % nx], rx.at[d - 1], xs_send.at[d - 1], xs_recv.at[d - 1], xpeer(d), me)

    def zs_copy(d):
        return remote(sx.at[(z + d) % nz], rz.at[d - 1], zs_send.at[d - 1], zs_recv.at[d - 1], zpeer(d), me)

    def zg_copy(d, src):
        return remote(vall.at[x, src], vall.at[x, src], zg_send.at[d - 1], zg_recv.at[d - 1], zpeer(d), me)

    def xg_copy(d, row, p):
        return remote(vall.at[row, p], vall.at[row, p], xg_send.at[d - 1, p], xg_recv.at[d - 1, p], xpeer(d), me)

    for d in range(1, nx):
        xs_copy(d).start()

    def own_turn(p, c):
        turn(win_v, own0 + 2 * p, v_buf[2 * p], v_buf[2 * p + 1])
        return c

    lax.fori_loop(0, nb // 2, own_turn, 0)

    for d in range(1, nx):
        xs_copy(d).wait_recv()
    sx[...] = ext[x]
    for d in range(1, nx):
        sx[...] = sx[...] + rx[d - 1]
    for d in range(1, nz):
        zs_copy(d).start()
    @pl.when(z == nz - 1)
    def _():
        for k in order:
            send_own(k)

    @pl.when(z != nz - 1)
    def _():
        for k in order[4:5]:
            send_own(k)

    a_copy(0).wait_recv()
    a_copy(1).wait_recv()
    b_copy().start()
    for d in range(1, nz):
        zs_copy(d).wait_recv()
    piece = sx[z]
    for d in range(1, nz):
        piece = piece + rz[d - 1]
    vall[x, z] = piece
    for d in range(1, nz):
        zg_copy(d, z).start()
    for d in range(1, nx):
        xg_copy(d, x, z).start()
    @pl.when(z != nz - 1)
    def _():
        for k in order[5:]:
            send_own(k)


    def take(j, c):
        k = nh - 1 - j
        own_copy(k, 0).wait_recv()
        own_copy(k, 1).wait_recv()

        @pl.when(z != nz - 1)
        def _():
            fwd_copy(k).start()

        @pl.when(z == nz - 1)
        def _():
            turn_copy(k).start()

        place(land1, k, nb)

        @pl.when(j >= lag)
        def _():
            relay(k + lag)

        return c

    lag = 3
    early = min(2, nh - 1)
    lax.fori_loop(0, early, take, 0)
    for d in range(1, nz):
        src = (z + nz - d) % nz
        zg_copy(d, src).wait_recv()
        for e in range(1, nx):
            xg_copy(e, x, src).start()
    b_copy().wait_recv()
    c_copy().start()
    lax.fori_loop(early, nh - 1, take, 0)

    for d in range(1, nx):
        row = (x + nx - d) % nx
        for p in range(nz):
            xg_copy(d, row, p).wait_recv()
    for part in range(nx):
        vturn[part] = vall[part, per:2 * per].reshape(per * BLK, HD).T
    load_q.wait()
    c_copy().wait_recv()
    place(land1, 0, nb)

    factor = math.log2(math.e) / math.sqrt(HD)
    nt = (((1,), (1,)), ((), ()))
    key_at = lax.broadcasted_iota(jnp.int32, (BLK, qrows), 0)
    row_at = lax.broadcasted_iota(jnp.int32, (BLK, qrows), 1) % BLK
    lanes = lax.broadcasted_iota(jnp.int32, (HD, 2 * BLK), 1)
    low = jnp.where(lanes < BLK, 1.0, 0.0).astype(BF16)
    high = jnp.where(lanes < BLK, 0.0, 1.0).astype(BF16)

    def offset(n):
        first = slash[0, 0]
        own = slash[0, n]
        return jnp.int32(0) if n == 0 else jnp.where(own == 0, first, own)

    tiles = [(g, per) for g in range(nx)] + [(nx + g, group) for g in range(ns // group)]
    starts = [sum(w for _, w in tiles[:t]) for t in range(len(tiles))]

    def scorer(r, buf, slot):
        q = q_buf[pl.ds(pl.multiple_of(r * BLK, BLK), BLK), :]
        qs = jnp.concatenate([q[:, h * HD:(h + 1) * HD] for h in range(hq)], axis=0)
        i = ctx * nb + r
        state = [jnp.full((8, qrows), NEG, F32)]

        def tile(t):
            g, width = tiles[t]
            if g < nx:
                kk = vall[g, 0:per].reshape(per * BLK, HD)
            else:
                kk = jnp.concatenate([win_k[r + own0 - offset((g - nx) * group + n)] for n in range(group)], axis=0)
            s = lax.dot_general(kk, qs, nt, preferred_element_type=F32)
            for n in range(width):
                at = starts[t] + n
                block = s[n * BLK:(n + 1) * BLK]
                if g < nx:
                    shift = jnp.where(vert[0, at] < i, 0.0, NEG)
                elif at == nv:
                    block = jnp.where(key_at > row_at, NEG, block)
                    shift = jnp.float32(0.0)
                else:
                    target = i - offset(at - nv)
                    bad = target < 0
                    for m in range(nv):
                        bad = bad | (target == vert[0, m])
                    shift = jnp.where(bad, NEG, 0.0)
                shifts[slot, at] = shift
                buf[at * BLK:(at + 1) * BLK, :] = block
                state[0] = jnp.maximum(state[0], jnp.max(block.reshape(BLK // 8, 8, qrows), axis=0) + shift)

        def done():
            tops[slot] = jnp.broadcast_to(jnp.max(state[0], axis=0, keepdims=True) * factor, (8, qrows))

        return tile, done

    def weigher(r, buf, slot):
        top = tops[slot, 0:1]
        state = [jnp.zeros((8, qrows), F32), jnp.zeros((HD, qrows), F32)]

        def tile(t):
            g, width = tiles[t]
            ws = []
            for n in range(width):
                at = starts[t] + n
                w = jnp.exp2(buf[at * BLK:(at + 1) * BLK, :] * factor - (top - shifts[slot, at]))
                state[0] = state[0] + jnp.sum(w.reshape(BLK // 8, 8, qrows), axis=0)
                ws.append(w.astype(BF16))
            w = jnp.concatenate(ws, axis=0)
            if g < nx:
                vt = vturn[g]
            else:
                pairs = []
                for n in range(0, group, 2):
                    one = r + own0 - offset((g - nx) * group + n)
                    two = r + own0 - offset((g - nx) * group + n + 1)
                    pairs.append(win_v[one] * low + win_v[two ^ 1] * high)
                vt = jnp.concatenate(pairs, axis=1)
            state[1] = state[1] + jnp.dot(vt, w, preferred_element_type=F32)

        def done():
            o = (state[1] / jnp.sum(state[0], axis=0, keepdims=True)).T.astype(BF16)
            for h in range(hq):
                stage[r // bpc, pl.ds(pl.multiple_of((r % bpc) * BLK, BLK), BLK), h * HD:(h + 1) * HD] = o[h * BLK:(h + 1) * BLK]

        return tile, done

    def both(r_next, buf_next, slot_next, r, buf, slot):
        score, score_done = scorer(r_next, buf_next, slot_next)
        weigh, weigh_done = weigher(r, buf, slot)
        for t in range(len(tiles)):
            score(t)
            weigh(t)
        score_done()
        weigh_done()

    def out_copy(ch):
        return remote(stage.at[ch], out_ref.at[:, pl.ds(pl.multiple_of(me * cols, cols), cols)], out_send.at[ch],
                      out_recv.at[me], ctx, ch)

    def out_arrival(src):
        return remote(stage.at[src], out_ref.at[:, pl.ds(pl.multiple_of(src * cols, cols), cols)], out_send.at[src],
                      out_recv.at[src], ctx, src)

    def out_local():
        return pltpu.make_async_copy(stage.at[me], out_ref.at[:, pl.ds(pl.multiple_of(me * cols, cols), cols)], loc_sem.at[3])

    last = nb - 1
    held = max(0, nh - 1 - lag)
    fwd_copy(nh - 1).wait_recv()
    place(land2, nh - 1, 0)
    score, score_done = scorer(last, buf_a, 0)
    for t in range(len(tiles)):
        score(t)
    score_done()

    def two_blocks(u, carry):
        odd = last - 2 * u

        @pl.when((u % 2 == 0) & (u >= 2) & (u // 2 <= nh - 1 - held))
        def _():
            relay(nh - held - u // 2)

        both(odd - 1, buf_b, 1, odd, buf_a, 0)
        even = odd - 1
        ch = even // bpc
        ends = even % bpc == 0

        @pl.when(ends & (ch > 1))
        def _():
            fwd_copy(ch - 1).wait_recv()

        @pl.when(ends & (ch > 0))
        def _():
            place(land2, ch - 1, 0)

        both(jnp.maximum(even - 1, 0), buf_a, 0, even, buf_b, 1)

        @pl.when(ends & (ch != me))
        def _():
            out_copy(ch).start()

        @pl.when(ends & (ch == me))
        def _():
            out_local().start()

        return carry

    lax.fori_loop(0, nb // 2, two_blocks, 0)

    for k in range(1, nh):
        own_copy(k, 0).wait_send()
        own_copy(k, 1).wait_send()
        fwd_copy(k).wait_send()

        @pl.when(z == nz - 1)
        def _(k=k):
            relay_copy(k).wait_send()
    a_copy(0).wait_send()
    a_copy(1).wait_send()
    b_copy().wait_send()
    c_copy().wait_send()
    for d in range(1, nx):
        xs_copy(d).wait_send()
        for p in range(nz):
            xg_copy(d, x, p).wait_send()
    for d in range(1, nz):
        zs_copy(d).wait_send()
        zg_copy(d, z).wait_send()
    for ch in range(nh):
        @pl.when(ch != me)
        def _(ch=ch):
            out_copy(ch).wait_send()
            out_arrival(ch).wait_recv()
    out_local().wait()


def solution(mesh, nx=NX):
    nh = mesh.shape["head"]
    nctx = mesh.shape["ctx"]
    nz = nctx // nx

    def local(queries, keys, values, vertical, slash):
        tok, qcols = queries.shape
        hq = qcols // HD
        nb = tok // BLK
        nv = vertical.shape[1]
        ns = slash.shape[1]
        assert 2 * nv == nx * nz
        cfg = (nx, nz, nh, nv, ns, nb, hq)
        rows = tok // nh
        per = nv // nx
        dma = pltpu.SemaphoreType.DMA
        hbm = pl.BlockSpec(memory_space=pl.ANY)
        smem = pl.BlockSpec(memory_space=pltpu.SMEM)
        return pl.pallas_call(
            functools.partial(kernel, cfg),
            out_shape=jax.ShapeDtypeStruct((rows, nh * qcols), BF16),
            in_specs=[smem, smem, hbm, hbm, hbm],
            out_specs=hbm,
            scratch_shapes=[
                pltpu.VMEM((tok, qcols), BF16),
                pltpu.VMEM((nb, BLK, HD), BF16),
                pltpu.VMEM(((LOOK + 1) * nb, BLK, HD), BF16),
                pltpu.VMEM(((LOOK + 1) * nb, HD, 2 * BLK), BF16),
                pltpu.VMEM((nh, 2, nb // nh, BLK, HD), BF16),
                pltpu.VMEM((nh, 2, nb // nh, BLK, HD), BF16),
                pltpu.VMEM((2, nb // nh, BLK, HD), BF16),
                pltpu.VMEM((nh, 2, nb // nh, BLK, HD), BF16),
                pltpu.VMEM((nx, nz, BLK, HD), BF16),
                pltpu.VMEM((nx - 1, nz, BLK, HD), BF16),
                pltpu.VMEM((nz, BLK, HD), BF16),
                pltpu.VMEM((nz - 1, BLK, HD), BF16),
                pltpu.VMEM((nx, nz, BLK, HD), BF16),
                pltpu.VMEM((nx, HD, per * BLK), BF16),
                pltpu.VMEM((nh, rows, qcols), BF16),
                pltpu.VMEM(((nv + ns) * BLK, hq * BLK), F32),
                pltpu.VMEM(((nv + ns) * BLK, hq * BLK), F32),
                pltpu.VMEM((2, 8, hq * BLK), F32),
                pltpu.SMEM((2, nv + ns), F32),
                dma((nh, 2)), dma((nh, 2)), dma((nh,)), dma((nh,)), dma((2,)), dma((2,)), dma((2,)), dma((2,)), dma((nh,)), dma((nh,)),
                dma((nx - 1,)), dma((nx - 1,)), dma((nz - 1,)), dma((nz - 1,)),
                dma((nz - 1,)), dma((nz - 1,)), dma((nx - 1, nz)), dma((nx - 1, nz)),
                dma((nh,)), dma((nh,)), dma((4,)),
            ],
            compiler_params=pltpu.CompilerParams(collective_id=0, has_side_effects=True, vmem_limit_bytes=56 * 1024 * 1024),
        )(vertical, slash, queries, keys.reshape(nb, BLK, HD), values.reshape(nb, BLK, HD))

    in_specs = (P("ctx", "head"), P("ctx", "head"), P("ctx", "head"), P("head", None), P("head", None))
    return jax.shard_map(local, mesh=mesh, in_specs=in_specs, out_specs=P(("ctx", "head"), None), check_vma=False)
```
